512 devices in a mesh: dp: 8 (over z_lo, core), row: 8 (over y), col: 8 (over z_hi, x).
Axes of the slice: x: 4, y: 8, z: 8 (z_hi: 2, z_lo: 4; z = z_hi * 4 + z_lo), core: 2. Of those that a mesh axis runs over, the one named last changes fastest.
Arguments:
- inputs: bfloat16 [1536, 4096], P('dp', 'row'), may hold values from -6 to 6
- weight: bfloat16 [4096, 14336], P('row', 'col'), may hold values from -0.09375 to 0.09375
- cotangent: bfloat16 [1536, 14336], P(('dp', 'row'), 'col'), may hold values from -6 to 6
- anchor: bfloat16 [4096, 14336], P(('row', 'dp'), 'col'), may hold values from -0.09375 to 0.09375
- first_moment: float32 [4096, 14336], P(('row', 'dp'), 'col'), may hold values from -0.15625 to 0.15625
- second_moment: float32 [4096, 14336], P(('row', 'dp'), 'col'), may hold values from 1e-06 to 0.0001
Outputs:
- outputs: bfloat16 [1536, 14336], P(('dp', 'row'), 'col')
- input_grad: bfloat16 [1536, 4096], P(('dp', 'col'), 'row')
- new_weight: bfloat16 [4096, 14336], P(('row', 'dp'), 'col')
- new_first: float32 [4096, 14336], P(('row', 'dp'), 'col')
- new_second: float32 [4096, 14336], P(('row', 'dp'), 'col')
The draws below stay inside these ranges and needn't reach their ends.
All inputs are finite; a program needn't handle non-finite values.
Results may differ from the reference program's by a relative error of at most 0.013.
Values may be sent and summed in bfloat16 or wider, within the bound.
A program may use at most 64 MiB of HBM per device.

```python
import math
import jax
import jax.numpy as jnp
from jax import lax

D = 4096
F = 14336
TOK_DEV = 192
TOKENS = 1536
DR = 512
FC = 1792
N_DP = 8
N_ROW = 8
N_COL = 8


def steps_of(key, dims, shards, smallest, top_value):
    def one(dim, shards_of):
        steps = jax.random.uniform(jax.random.fold_in(jax.random.fold_in(key, 6), dim), (shards_of,), jnp.float32, smallest / len(shards), top_value / len(shards))
        return jnp.repeat(jnp.exp(steps), dims[dim] // shards_of).reshape((-1,) + (1,) * (len(dims) - dim - 1))

    gain = one(*shards[0])
    for cut in shards[1:]:
        gain = gain * one(*cut)
    return gain


def noise(key, extent, scale, limit, shards=(), kind=jnp.bfloat16):
    drawn = scale * jax.random.normal(key, extent, jnp.float32)
    if shards:
        drawn = drawn * steps_of(key, extent, shards, -0.22, 0.18)
    return jnp.clip(drawn, -limit, limit).astype(kind)


def setup_inputs(seed: int = 0) -> dict:
    seeds = jax.random.split(jax.random.key(seed), 7)
    inputs = noise(seeds[0], (TOKENS, D), 1.0, 6.0, ((0, 8), (1, 8)))
    weight = noise(seeds[1], (D, F), D ** -0.5, 0.09375, ((0, 8), (1, 8)))
    cotangent = noise(seeds[2], (TOKENS, F), 1.0, 6.0, ((0, 64), (1, 8)))
    anchor = noise(seeds[3], (D, F), D ** -0.5, 0.09375, ((0, 64), (1, 8)))
    first_moment = noise(seeds[4], (D, F), 0.01, 0.15625, ((0, 64), (1, 8)), jnp.float32)
    second_moment = jnp.clip(jnp.exp(math.log(0.0001) - 4.6051702 * jax.random.uniform(seeds[5], (D, F), jnp.float32) ** steps_of(seeds[5], (D, F), ((0, 64), (1, 8)), -0.2, 0.2)), 9.999999974752427e-07, 0.0001)
    return dict(inputs=inputs, weight=weight, cotangent=cotangent, anchor=anchor, first_moment=first_moment, second_moment=second_moment)


beta_one = 0.9
beta_two = 0.999
learn_rate = 0.002
anchor_pull = 0.5
epsilon = 1e-08
step_count = 100.0

def rounded(value):
    narrow = lax.optimization_barrier(value.astype(jnp.bfloat16))
    return narrow.astype(jnp.float32)

def reference(inputs, weight, cotangent, anchor, first_moment, second_moment):
    total = jnp.zeros((TOKENS, F), jnp.float32)
    for block in range(N_ROW):
        part = jnp.dot(inputs[:, block * DR:(block + 1) * DR], weight[block * DR:(block + 1) * DR, :], preferred_element_type=jnp.float32)
        total = total + rounded(part)
    outputs = total.astype(jnp.bfloat16)
    grad_total = jnp.zeros((TOKENS, D), jnp.float32)
    for block in range(N_COL):
        gpart = lax.dot_general(cotangent[:, block * FC:(block + 1) * FC], weight[:, block * FC:(block + 1) * FC], (((1,), (1,)), ((), ())), preferred_element_type=jnp.float32)
        grad_total = grad_total + rounded(gpart)
    input_grad = grad_total.astype(jnp.bfloat16)
    summed = jnp.zeros((D, F), jnp.float32)
    for block in range(N_DP):
        piece = lax.dot_general(inputs[block * TOK_DEV:(block + 1) * TOK_DEV, :], cotangent[block * TOK_DEV:(block + 1) * TOK_DEV, :], (((0,), (0,)), ((), ())), preferred_element_type=jnp.float32)
        summed = summed + rounded(piece)
    current = weight.astype(jnp.float32)
    grad = summed / TOKENS + anchor_pull * (current - anchor.astype(jnp.float32))
    new_first = beta_one * first_moment + (1.0 - beta_one) * grad
    new_second = beta_two * second_moment + (1.0 - beta_two) * grad * grad
    mhat = new_first / (1.0 - beta_one ** step_count)
    vhat = new_second / (1.0 - beta_two ** step_count)
    new_weight = (current - learn_rate * mhat / (jnp.sqrt(vhat) + epsilon)).astype(jnp.bfloat16)
    return (outputs, input_grad, new_weight, new_first, new_second)
```

```python
import functools

import jax
import jax.numpy as jnp
from jax import lax
from jax.experimental import pallas as pl
from jax.experimental.pallas import tpu as pltpu
from jax.sharding import PartitionSpec as P

beta_one = 0.9
beta_two = 0.999
learn_rate = 0.002
anchor_pull = 0.5
epsilon = 1e-08
step_count = 100.0

MESH = pl.DeviceIdType.MESH
f32, bf16 = jnp.float32, jnp.bfloat16
NZ = 4


def chunks_of(width):
    if width == 1792:
        sizes = (256, 512, 512, 512)
    else:
        sizes = (128,) * (width // 128)
    out, at = [], 0
    for size in sizes:
        out.append((at, size))
        at += size
    return out


def kernel(
    n_row, n_x, n_zh, tokens,
    x_ref, w_ref, ct_ref, an_ref, m_ref, v_ref,
    out_ref, ig_ref, nw_ref, nm_ref, nv_ref,
    xv, xpv, wv, ctb, ctp, xts, xs, xps, pb, rsr, gacc, gp, xr, zhs, zhr,
    zs, zr, acc, anv, mv, vv, outv, igv, nwv, nmv, nvv,
    load_sem, store_sem, x_sem, core_send, core_recv, ag_send, ag_recv, rs_send, rs_recv,
    z_send, z_recv, gx_send, gx_recv, zh_sem,
):
    width = w_ref.shape[1]
    T, DR = x_ref.shape
    blocks_of_rows = 2 * NZ
    own = DR // blocks_of_rows
    chunks = chunks_of(width)
    nk = len(chunks)
    dp, r, q = lax.axis_index("dp"), lax.axis_index("row"), lax.axis_index("col")
    z, c = dp // 2, dp % 2
    zh, xx = q // n_x, q % n_x
    right, left = lax.rem(r + 1, n_row), lax.rem(r + n_row - 1, n_row)
    ring = (right, left)
    sign = (1, -1)
    partner = 2 * z + (1 - c)

    def at_row(offset):
        return lax.rem(r + offset + 2 * n_row, n_row)

    def remote(src, dst, ssem, rsem, **device):
        return pltpu.make_async_remote_copy(
            src_ref=src, dst_ref=dst, send_sem=ssem, recv_sem=rsem,
            device_id=device, device_id_type=MESH,
        )

    barrier = pltpu.get_barrier_semaphore()
    greet = [dict(row=right), dict(row=left), dict(dp=partner)]
    for j in range(1, n_x):
        greet.append(dict(col=zh * n_x + lax.rem(xx + j, n_x)))
    if n_zh == 2:
        greet.append(dict(col=(1 - zh) * n_x + xx))
    for device in greet:
        pl.semaphore_signal(barrier, inc=1, device_id=device, device_id_type=MESH)
    for d in range(NZ):
        @pl.when((z != d) & (z + 3 != d) & (z != d + 3))
        def _():
            pl.semaphore_signal(barrier, inc=1, device_id=dict(dp=2 * d + c), device_id_type=MESH)

    loads = [
        pltpu.make_async_copy(x_ref, xv, load_sem.at[0]),
        pltpu.make_async_copy(w_ref, wv, load_sem.at[1]),
        pltpu.make_async_copy(ct_ref, ctb.at[r], load_sem.at[2]),
        pltpu.make_async_copy(m_ref, mv, load_sem.at[3]),
        pltpu.make_async_copy(v_ref, vv, load_sem.at[4]),
        pltpu.make_async_copy(an_ref, anv, load_sem.at[5]),
    ]
    for i in (2, 0, 1, 3, 4, 5):
        loads[i].start()

    def select(src, dst):
        xts[...] = src[...].T.reshape(NZ, 2, own, T)
        dst[...] = xts[:, c].reshape(NZ * own, T)

    loads[0].wait()
    select(xv, xs)
    loads[2].wait()
    pl.semaphore_wait(barrier, len(greet) + 2 + jnp.where((z == 1) | (z == 2), 1, 0))

    sends = []

    def go(copy):
        copy.start()
        sends.append(copy)

    def steps_of(k, d):
        return n_row // 2 if (k + d) % 2 == 0 else (n_row - 1) // 2

    def ag_copy(k, d, hop, receiving):
        cols = pl.ds(chunks[k][0], chunks[k][1])
        block = at_row(-sign[d] * (hop + (1 if receiving else 0)))
        view = ctb.at[block, :, :, cols]
        return remote(view, view, ag_send.at[k, d, hop], ag_recv.at[k, d, hop], row=ring[d])

    def core_copy(k, offset):
        cols = pl.ds(chunks[k][0], chunks[k][1])
        block = at_row(offset)
        slot = offset % n_row
        return remote(
            ctb.at[block, :, :, cols], ctp.at[block, :, :, cols],
            core_send.at[k, slot], core_recv.at[k, slot], dp=partner,
        )

    x_copy = remote(xv, xpv, x_sem.at[0], x_sem.at[1], dp=partner)
    for k in range(nk):
        for d in range(2):
            if steps_of(k, d):
                go(ag_copy(k, d, 0, False))
        if k == 0:
            go(x_copy)
        go(core_copy(k, 0))

    loads[1].wait()
    for at, size in chunks:
        part = jnp.dot(xv[...], wv[:, at:at + size], preferred_element_type=f32)
        pb[:, :, :, at:at + size] = part.reshape(n_row, 3, 8, size).astype(bf16)

    x_copy.wait_recv()
    select(xpv, xps)

    def gather(k):
        for hop in range(n_row // 2):
            for d in range(2):
                if hop < steps_of(k, d):
                    ag_copy(k, d, hop, True).wait_recv()
                    if hop + 1 < steps_of(k, d):
                        go(ag_copy(k, d, hop + 1, False))
                    go(core_copy(k, -sign[d] * (hop + 1)))

    def rows_of(ref, at, size):
        return ref[:, :, :, at:at + size].astype(f32).reshape(T, size).astype(bf16)

    def multiply(k):
        at, size = chunks[k]
        for slot in range(n_row):
            core_copy(k, slot).wait_recv()
        mine = rows_of(ctb, at, size)
        other = rows_of(ctp, at, size)
        grad = jnp.dot(xs[...], mine, preferred_element_type=f32)
        grad = grad + jnp.dot(xps[...], other, preferred_element_type=f32)
        zs[:, :, at:at + size] = grad.reshape(NZ, own, size).astype(bf16)
        return mine

    def input_part(k, mine):
        at, size = chunks[k]
        part = lax.dot_general(
            mine, wv[:, at:at + size], (((1,), (1,)), ((), ())), preferred_element_type=f32
        )
        gacc[...] = part if k == 0 else gacc[...] + part

    def z_copy(k, source, target, slot):
        cols = pl.ds(chunks[k][0], chunks[k][1])
        return remote(
            zs.at[target, :, cols], zr.at[slot, :, cols],
            z_send.at[k, target], z_recv.at[k, slot], dp=2 * source + c,
        )

    def is_relay(d):
        return (z == 1) if d == 3 else (z == 2) if d == 0 else None

    def z_direct(k):
        for d, end, via in ((3, 0, 1), (0, 3, 2)):
            @pl.when(z == end)
            def _():
                z_copy(k, via, d, NZ).start()
        for d in (2, 1, 0, 3):
            ok = z != d
            if d == 3:
                ok = z == 2
            if d == 0:
                ok = z == 1
            @pl.when(ok)
            def _():
                z_copy(k, d, d, z).start()

    def z_relay(k):
        at, size = chunks[k]
        for d, via in ((3, 1), (0, 2)):
            @pl.when(z == via)
            def _():
                z_copy(k, d, d, NZ).wait_recv()
                both = zs[d, :, at:at + size].astype(f32) + zr[NZ, :, at:at + size].astype(f32)
                zs[d, :, at:at + size] = both.astype(bf16)
                z_copy(k, d, d, z).start()

    def z_wait_sends(k):
        for d in range(NZ):
            @pl.when(z != d)
            def _():
                z_copy(k, d, d, 0).wait_send()

    stores = []

    def put(src, dst, sem):
        copy = pltpu.make_async_copy(src, dst, sem)
        copy.start()
        stores.append(copy)

    def update(k):
        at, size = chunks[k]
        cols = pl.ds(at, size)
        acc[:, :size] = zs[z, :, at:at + size].astype(f32)
        for s in range(NZ):
            @pl.when((z != s) & (z + 3 != s) & (z != s + 3))
            def _():
                z_copy(k, s, s, s).wait_recv()
                acc[:, :size] += zr[s, :, at:at + size].astype(f32)
        rows = pl.ds(pl.multiple_of(dp * own, own), own)
        current = wv[rows, at:at + size].astype(f32)
        grad = acc[:, :size] * (1.0 / tokens) + anchor_pull * (current - anv[:, at:at + size].astype(f32))
        first = beta_one * mv[:, at:at + size] + (1.0 - beta_one) * grad
        second = beta_two * vv[:, at:at + size] + (1.0 - beta_two) * grad * grad
        nmv[:, at:at + size] = first
        nvv[:, at:at + size] = second
        put(nmv.at[:, cols], nm_ref.at[:, cols], store_sem.at[k, 0])
        put(nvv.at[:, cols], nv_ref.at[:, cols], store_sem.at[k, 1])
        mhat = first * (1.0 / (1.0 - beta_one**step_count))
        vhat = second * (1.0 / (1.0 - beta_two**step_count))
        nwv[:, at:at + size] = (current - learn_rate * mhat / (jnp.sqrt(vhat) + epsilon)).astype(bf16)
        put(nwv.at[:, cols], nw_ref.at[:, cols], store_sem.at[k, 2])

    half = width // 2

    def rs_copy(h, d, step, receiving):
        total = steps_of(h, d)
        cols = pl.ds(h * half, half)
        target = at_row(sign[d] * (total - step - (1 if receiving else 0)))
        return remote(
            pb.at[target, :, :, cols], rsr.at[d, step, :, :, cols],
            rs_send.at[h, d, step], rs_recv.at[h, d, step], row=ring[d],
        )

    def rs_step(step):
        for h in range(2):
            for d in range(2):
                total = steps_of(h, d)
                cols = slice(h * half, (h + 1) * half)
                if step and step <= total:
                    rs_copy(h, d, step - 1, True).wait_recv()
                    if step < total:
                        block = at_row(sign[d] * (total - step))
                        both = pb[block, :, :, cols].astype(f32) + rsr[d, step - 1, :, :, cols].astype(f32)
                        pb[block, :, :, cols] = both.astype(bf16)
                if step < total:
                    go(rs_copy(h, d, step, False))

    def rs_finish():
        for h in range(2):
            cols = slice(h * half, (h + 1) * half)
            total = pb[r, :, :, cols].astype(f32)
            for d in range(2):
                if steps_of(h, d):
                    total = total + rsr[d, steps_of(h, d) - 1, :, :, cols].astype(f32)
            outv[:, :, cols] = total.astype(bf16)
        put(outv, out_ref, store_sem.at[nk, 0])

    def gx_copy(j):
        target = lax.rem(xx + j, n_x)
        return remote(
            gp.at[:, target], xr.at[j - 1], gx_send.at[j - 1], gx_recv.at[j - 1],
            col=zh * n_x + target,
        )

    def gx_start():
        gp[...] = gacc[...].reshape(n_zh, n_x, 3, 8, DR).astype(bf16)
        for j in range(1, n_x):
            go(gx_copy(j))

    def zh_copy():
        return remote(zhs, zhr, zh_sem.at[0], zh_sem.at[1], col=(1 - zh) * n_x + xx)

    def gx_finish():
        for j in range(1, n_x):
            gx_copy(j).wait_recv()

        def total(side):
            out = gp[side, xx].astype(f32)
            for j in range(1, n_x):
                out = out + xr[j - 1, side].astype(f32)
            return out

        if n_zh == 2:
            zhs[...] = total(1 - zh).astype(bf16)
            go(zh_copy())
        igv[...] = total(zh).astype(bf16)

    def ig_finish():
        if n_zh == 2:
            zh_copy().wait_recv()
            igv[...] = (igv[...].astype(f32) + zhr[...].astype(f32)).astype(bf16)
        put(igv, ig_ref, store_sem.at[nk, 1])

    rs_total = n_row // 2
    rs_next = 0
    for k in range(nk):
        gather(k)
        mine = multiply(k)
        z_direct(k)
        input_part(k, mine)
        if k:
            z_relay(k - 1)
        if k >= nk - 2:
            rs_step(rs_next)
            rs_next += 1
    gx_start()
    rs_step(rs_next)
    rs_next += 1
    z_relay(nk - 1)
    gx_finish()
    for i in (3, 4, 5):
        loads[i].wait()
    update(0)
    while rs_next <= rs_total:
        rs_step(rs_next)
        rs_next += 1
    for k in range(1, nk - 1):
        update(k)
    rs_finish()
    ig_finish()
    update(nk - 1)

    for copy in sends:
        copy.wait_send()
    for k in range(nk):
        z_wait_sends(k)
    for copy in stores:
        copy.wait()


def make_per_device(n_row, n_x, n_zh, n_dp=8):
    def per_device(inputs, weight, cotangent, anchor, first_moment, second_moment):
        T, DR = inputs.shape
        width = weight.shape[1]
        own = DR // n_dp
        nk = len(chunks_of(width))
        hops = max(n_row // 2, 1)
        tall = cotangent.reshape(3, 8, width)
        dma = pltpu.SemaphoreType.DMA
        V = pltpu.VMEM
        scratch = [
            V((T, DR), bf16), V((T, DR), bf16), V((DR, width), bf16),
            V((n_row, 3, 8, width), bf16), V((n_row, 3, 8, width), bf16),
            V((NZ, 2, own, T), bf16), V((NZ * own, T), bf16), V((NZ * own, T), bf16),
            V((n_row, 3, 8, width), bf16), V((2, hops, 3, 8, width), bf16),
            V((T, DR), f32), V((n_zh, n_x, 3, 8, DR), bf16), V((n_x - 1, n_zh, 3, 8, DR), bf16),
            V((3, 8, DR), bf16), V((3, 8, DR), bf16),
            V((NZ, own, width), bf16), V((NZ + 1, own, width), bf16), V((own, 512), f32),
            V((own, width), bf16), V((own, width), f32), V((own, width), f32),
            V((3, 8, width), bf16), V((3, 8, DR), bf16),
            V((own, width), bf16), V((own, width), f32), V((own, width), f32),
            dma((6,)), dma((nk + 1, 3)), dma((2,)),
            dma((nk, n_row)), dma((nk, n_row)),
            dma((nk, 2, hops)), dma((nk, 2, hops)),
            dma((2, 2, hops)), dma((2, 2, hops)),
            dma((nk, NZ)), dma((nk, NZ + 1)),
            dma((n_x - 1,)), dma((n_x - 1,)), dma((2,)),
        ]
        hbm = pl.BlockSpec(memory_space=pl.ANY)
        out, ig, nw, nm, nv = pl.pallas_call(
            functools.partial(kernel, n_row, n_x, n_zh, T * n_dp),
            out_shape=(
                jax.ShapeDtypeStruct((3, 8, width), bf16),
                jax.ShapeDtypeStruct((3, 8, DR), bf16),
                jax.ShapeDtypeStruct((own, width), bf16),
                jax.ShapeDtypeStruct((own, width), f32),
                jax.ShapeDtypeStruct((own, width), f32),
            ),
            in_specs=[hbm] * 6,
            out_specs=(hbm,) * 5,
            scratch_shapes=scratch,
            compiler_params=pltpu.CompilerParams(
                collective_id=0, has_side_effects=True, vmem_limit_bytes=48 * 1024 * 1024
            ),
        )(inputs, weight, tall, anchor, first_moment, second_moment)
        return out.reshape(24, width), ig.reshape(24, DR), nw, nm, nv

    return per_device


def solution(mesh):
    in_specs = (
        P("dp", "row"),
        P("row", "col"),
        P(("dp", "row"), "col"),
        P(("row", "dp"), "col"),
        P(("row", "dp"), "col"),
        P(("row", "dp"), "col"),
    )
    out_specs = (
        P(("dp", "row"), "col"),
        P(("dp", "col"), "row"),
        P(("row", "dp"), "col"),
        P(("row", "dp"), "col"),
        P(("row", "dp"), "col"),
    )
    n_row, n_col = mesh.shape["row"], mesh.shape["col"]
    n_zh = 2 if n_col > 2 else 1
    return jax.shard_map(
        make_per_device(n_row, n_col // n_zh, n_zh), mesh=mesh,
        in_specs=in_specs, out_specs=out_specs, check_vma=False,
    )
```

```python
import functools

import jax
import jax.numpy as jnp
from jax import lax
from jax.experimental import pallas as pl
from jax.experimental.pallas import tpu as pltpu
from jax.sharding import PartitionSpec as P

beta_one = 0.9
beta_two = 0.999
learn_rate = 0.002
anchor_pull = 0.5
epsilon = 1e-08
step_count = 100.0

MESH = pl.DeviceIdType.MESH
f32, bf16 = jnp.float32, jnp.bfloat16
NZ = 4


def chunks_of(width):
    if width == 1792:
        sizes = (256, 512, 512, 512)
    else:
        sizes = (128,) * (width // 128)
    out, at = [], 0
    for size in sizes:
        out.append((at, size))
        at += size
    return out


def kernel(
    n_row, n_x, n_zh, tokens,
    x_ref, w_ref, ct_ref, an_ref, m_ref, v_ref,
    out_ref, ig_ref, nw_ref, nm_ref, nv_ref,
    xv, xpv, wv, ctb, ctp, xts, xs, xps, pb, rsr, gacc, gp, xr, zhs, zhr,
    zs, zr, acc, anv, mv, vv, outv, igv, nwv, nmv, nvv,
    load_sem, store_sem, x_sem, core_send, core_recv, ag_send, ag_recv, rs_send, rs_recv,
    z_send, z_recv, gx_send, gx_recv, zh_sem,
):
    width = w_ref.shape[1]
    T, DR = x_ref.shape
    blocks_of_rows = 2 * NZ
    own = DR // blocks_of_rows
    chunks = chunks_of(width)
    nk = len(chunks)
    dp, r, q = lax.axis_index("dp"), lax.axis_index("row"), lax.axis_index("col")
    z, c = dp // 2, dp % 2
    zh, xx = q // n_x, q % n_x
    right, left = lax.rem(r + 1, n_row), lax.rem(r + n_row - 1, n_row)
    ring = (right, left)
    sign = (1, -1)
    partner = 2 * z + (1 - c)

    def at_row(offset):
        return lax.rem(r + offset + 2 * n_row, n_row)

    def remote(src, dst, ssem, rsem, **device):
        return pltpu.make_async_remote_copy(
            src_ref=src, dst_ref=dst, send_sem=ssem, recv_sem=rsem,
            device_id=device, device_id_type=MESH,
        )

    barrier = pltpu.get_barrier_semaphore()
    greet = [dict(row=right), dict(row=left), dict(dp=partner)]
    for j in range(1, n_x):
        greet.append(dict(col=zh * n_x + lax.rem(xx + j, n_x)))
    if n_zh == 2:
        greet.append(dict(col=(1 - zh) * n_x + xx))
    for device in greet:
        pl.semaphore_signal(barrier, inc=1, device_id=device, device_id_type=MESH)
    for step, inner in ((1, z < NZ - 1), (-1, z > 0)):
        @pl.when(inner)
        def _():
            pl.semaphore_signal(
                barrier, inc=1, device_id=dict(dp=2 * (z + step) + c), device_id_type=MESH
            )

    loads = [
        pltpu.make_async_copy(x_ref, xv, load_sem.at[0]),
        pltpu.make_async_copy(w_ref, wv, load_sem.at[1]),
        pltpu.make_async_copy(ct_ref, ctb.at[r], load_sem.at[2]),
        pltpu.make_async_copy(m_ref, mv, load_sem.at[3]),
        pltpu.make_async_copy(v_ref, vv, load_sem.at[4]),
        pltpu.make_async_copy(an_ref, anv, load_sem.at[5]),
    ]
    for i in (2, 0, 1, 3, 4, 5):
        loads[i].start()

    def select(src, dst):
        xts[...] = src[...].T.reshape(NZ, 2, own, T)
        dst[...] = xts[:, c].reshape(NZ * own, T)

    loads[0].wait()
    select(xv, xs)
    loads[2].wait()
    pl.semaphore_wait(barrier, len(greet) + 1 + jnp.where((z == 1) | (z == 2), 1, 0))

    sends = []

    def go(copy):
        copy.start()
        sends.append(copy)

    def steps_of(k, d):
        return n_row // 2 if (k + d) % 2 == 0 else (n_row - 1) // 2

    def ag_copy(k, d, hop, receiving):
        cols = pl.ds(chunks[k][0], chunks[k][1])
        block = at_row(-sign[d] * (hop + (1 if receiving else 0)))
        view = ctb.at[block, :, :, cols]
        return remote(view, view, ag_send.at[k, d, hop], ag_recv.at[k, d, hop], row=ring[d])

    def core_copy(k, offset):
        cols = pl.ds(chunks[k][0], chunks[k][1])
        block = at_row(offset)
        slot = offset % n_row
        return remote(
            ctb.at[block, :, :, cols], ctp.at[block, :, :, cols],
            core_send.at[k, slot], core_recv.at[k, slot], dp=partner,
        )

    x_copy = remote(xv, xpv, x_sem.at[0], x_sem.at[1], dp=partner)
    for k in range(nk):
        for d in range(2):
            if steps_of(k, d):
                go(ag_copy(k, d, 0, False))
        if k == 0:
            go(x_copy)
        go(core_copy(k, 0))

    loads[1].wait()
    for at, size in chunks:
        part = jnp.dot(xv[...], wv[:, at:at + size], preferred_element_type=f32)
        pb[:, :, :, at:at + size] = part.reshape(n_row, 3, 8, size).astype(bf16)

    def gather(k, hop):
        for d in range(2):
            if hop < steps_of(k, d):
                ag_copy(k, d, hop, True).wait_recv()
                if hop + 1 < steps_of(k, d):
                    go(ag_copy(k, d, hop + 1, False))
                go(core_copy(k, -sign[d] * (hop + 1)))

    def rows_of(ref, at, size):
        return ref[:, :, :, at:at + size].astype(f32).reshape(T, size).astype(bf16)

    def multiply(k):
        at, size = chunks[k]
        for slot in range(n_row):
            core_copy(k, slot).wait_recv()
        mine = rows_of(ctb, at, size)
        other = rows_of(ctp, at, size)
        grad = jnp.dot(xs[...], mine, preferred_element_type=f32)
        grad = grad + jnp.dot(xps[...], other, preferred_element_type=f32)
        zs[:, :, at:at + size] = grad.reshape(NZ, own, size).astype(bf16)
        return mine

    def input_part(k, mine):
        at, size = chunks[k]
        part = lax.dot_general(
            mine, wv[:, at:at + size], (((1,), (1,)), ((), ())), preferred_element_type=f32
        )
        gacc[...] = part if k == 0 else gacc[...] + part

    def z_copy(k, way, d):
        cols = pl.ds(chunks[k][0], chunks[k][1])
        to = jnp.minimum(z + 1, NZ - 1) if way == 0 else jnp.maximum(z - 1, 0)
        return remote(
            zs.at[d, :, cols], zr.at[way, d, :, cols],
            z_send.at[k, d], z_recv.at[way, k, d], dp=2 * to + c,
        )

    def z_first(k, hops):
        for way, at_z, d in ((0, 0, hops), (1, NZ - 1, NZ - 1 - hops)):
            @pl.when(z == at_z)
            def _():
                z_copy(k, way, d).start()

    def z_relay(k, at_end, left):
        at, size = chunks[k]
        for way in range(2):
            here = at_end if way == 0 else NZ - 1 - at_end
            d = here + left if way == 0 else here - left

            @pl.when(z == here)
            def _():
                z_copy(k, way, d).wait_recv()
                both = zs[d, :, at:at + size].astype(f32) + zr[way, d, :, at:at + size].astype(f32)
                zs[d, :, at:at + size] = both.astype(bf16)
                z_copy(k, way, d).start()

    def z_wait_sends(k):
        for d in range(NZ):
            @pl.when(z != d)
            def _():
                z_copy(k, 0, d).wait_send()

    stores = []

    def put(src, dst, sem):
        copy = pltpu.make_async_copy(src, dst, sem)
        copy.start()
        stores.append(copy)

    def update(k):
        at, size = chunks[k]
        cols = pl.ds(at, size)
        acc[:, :size] = zs[z, :, at:at + size].astype(f32)
        for way, inner in ((0, z > 0), (1, z < NZ - 1)):
            @pl.when(inner)
            def _():
                z_copy(k, way, z).wait_recv()
                acc[:, :size] += zr[way, z, :, at:at + size].astype(f32)
        rows = pl.ds(pl.multiple_of(dp * own, own), own)
        current = wv[rows, at:at + size].astype(f32)
        grad = acc[:, :size] * (1.0 / tokens) + anchor_pull * (current - anv[:, at:at + size].astype(f32))
        first = beta_one * mv[:, at:at + size] + (1.0 - beta_one) * grad
        second = beta_two * vv[:, at:at + size] + (1.0 - beta_two) * grad * grad
        nmv[:, at:at + size] = first
        nvv[:, at:at + size] = second
        put(nmv.at[:, cols], nm_ref.at[:, cols], store_sem.at[k, 0])
        put(nvv.at[:, cols], nv_ref.at[:, cols], store_sem.at[k, 1])
        mhat = first * (1.0 / (1.0 - beta_one**step_count))
        vhat = second * (1.0 / (1.0 - beta_two**step_count))
        nwv[:, at:at + size] = (current - learn_rate * mhat / (jnp.sqrt(vhat) + epsilon)).astype(bf16)
        put(nwv.at[:, cols], nw_ref.at[:, cols], store_sem.at[k, 2])

    half = width // 2

    def rs_copy(h, d, step, receiving):
        total = steps_of(h, d)
        cols = pl.ds(h * half, half)
        target = at_row(sign[d] * (total - step - (1 if receiving else 0)))
        return remote(
            pb.at[target, :, :, cols], rsr.at[d, step, :, :, cols],
            rs_send.at[h, d, step], rs_recv.at[h, d, step], row=ring[d],
        )

    def rs_step(step):
        for h in range(2):
            for d in range(2):
                total = steps_of(h, d)
                cols = slice(h * half, (h + 1) * half)
                if step and step <= total:
                    rs_copy(h, d, step - 1, True).wait_recv()
                    if step < total:
                        block = at_row(sign[d] * (total - step))
                        both = pb[block, :, :, cols].astype(f32) + rsr[d, step - 1, :, :, cols].astype(f32)
                        pb[block, :, :, cols] = both.astype(bf16)
                if step < total:
                    go(rs_copy(h, d, step, False))

    def rs_finish():
        for h in range(2):
            cols = slice(h * half, (h + 1) * half)
            total = pb[r, :, :, cols].astype(f32)
            for d in range(2):
                if steps_of(h, d):
                    total = total + rsr[d, steps_of(h, d) - 1, :, :, cols].astype(f32)
            outv[:, :, cols] = total.astype(bf16)
        put(outv, out_ref, store_sem.at[nk, 0])

    def gx_copy(j):
        target = lax.rem(xx + j, n_x)
        return remote(
            gp.at[:, target], xr.at[j - 1], gx_send.at[j - 1], gx_recv.at[j - 1],
            col=zh * n_x + target,
        )

    def gx_start():
        gp[...] = gacc[...].reshape(n_zh, n_x, 3, 8, DR).astype(bf16)
        for j in range(1, n_x):
            go(gx_copy(j))

    def zh_copy():
        return remote(zhs, zhr, zh_sem.at[0], zh_sem.at[1], col=(1 - zh) * n_x + xx)

    def gx_finish():
        for j in range(1, n_x):
            gx_copy(j).wait_recv()

        def total(side):
            out = gp[side, xx].astype(f32)
            for j in range(1, n_x):
                out = out + xr[j - 1, side].astype(f32)
            return out

        if n_zh == 2:
            zhs[...] = total(1 - zh).astype(bf16)
            go(zh_copy())
        igv[...] = total(zh).astype(bf16)

    def ig_finish():
        if n_zh == 2:
            zh_copy().wait_recv()
            igv[...] = (igv[...].astype(f32) + zhr[...].astype(f32)).astype(bf16)
        put(igv, ig_ref, store_sem.at[nk, 1])

    hops = n_row // 2
    far = NZ - 1

    def finish_chunk(k):
        mine = multiply(k)
        z_first(k, far)
        input_part(k, mine)

    for hop in range(hops):
        if hop == hops - 1:
            rs_step(0)
        for k in range(nk):
            gather(k, hop)
            if hop == hops - 1 and k:
                finish_chunk(k - 1)
        if hop == 0:
            x_copy.wait_recv()
            select(xpv, xps)
    finish_chunk(nk - 1)
    gx_start()
    for k in range(nk):
        z_first(k, 2)
    rs_step(1)
    for k in range(nk + 1):
        if k < nk:
            z_relay(k, 1, 2)
        if k == 2:
            rs_step(2)
        if k:
            z_relay(k - 1, 2, 1)
    gx_finish()
    for k in range(nk):
        z_first(k, 1)
    rs_step(3)
    for k in range(nk):
        z_relay(k, 1, 1)
    for i in (3, 4, 5):
        loads[i].wait()
    for step in range(4, hops + 1):
        rs_step(step)
    rs_finish()
    ig_finish()
    for k in range(nk):
        update(k)

    for copy in sends:
        copy.wait_send()
    for k in range(nk):
        z_wait_sends(k)
    for copy in stores:
        copy.wait()


def write_kernel(*refs):
    n = (len(refs) - 1) // 2
    copies = [pltpu.make_async_copy(refs[i], refs[n + i], refs[-1].at[i]) for i in range(n)]
    for copy in copies:
        copy.start()
    for copy in copies:
        copy.wait()


def write_out(*arrays):
    n = len(arrays)
    return pl.pallas_call(
        write_kernel,
        out_shape=tuple(jax.ShapeDtypeStruct(a.shape, a.dtype) for a in arrays),
        in_specs=[pl.BlockSpec(memory_space=pl.ANY)] * n,
        out_specs=(pl.BlockSpec(memory_space=pltpu.HBM),) * n,
        scratch_shapes=[pltpu.SemaphoreType.DMA((n,))],
        compiler_params=pltpu.CompilerParams(vmem_limit_bytes=4 * 1024 * 1024),
    )(*arrays)


def make_per_device(n_row, n_x, n_zh, n_dp=8):
    def per_device(inputs, weight, cotangent, anchor, first_moment, second_moment):
        T, DR = inputs.shape
        width = weight.shape[1]
        own = DR // n_dp
        nk = len(chunks_of(width))
        hops = max(n_row // 2, 1)
        tall = cotangent.reshape(3, 8, width)
        dma = pltpu.SemaphoreType.DMA
        V = pltpu.VMEM
        scratch = [
            V((T, DR), bf16), V((T, DR), bf16), V((DR, width), bf16),
            V((n_row, 3, 8, width), bf16), V((n_row, 3, 8, width), bf16),
            V((NZ, 2, own, T), bf16), V((NZ * own, T), bf16), V((NZ * own, T), bf16),
            V((n_row, 3, 8, width), bf16), V((2, hops, 3, 8, width), bf16),
            V((T, DR), f32), V((n_zh, n_x, 3, 8, DR), bf16), V((n_x - 1, n_zh, 3, 8, DR), bf16),
            V((3, 8, DR), bf16), V((3, 8, DR), bf16),
            V((NZ, own, width), bf16), V((2, NZ, own, width), bf16), V((own, 512), f32),
            V((own, width), bf16), V((own, width), f32), V((own, width), f32),
            V((3, 8, width), bf16), V((3, 8, DR), bf16),
            V((own, width), bf16), V((own, width), f32), V((own, width), f32),
            dma((6,)), dma((nk + 1, 3)), dma((2,)),
            dma((nk, n_row)), dma((nk, n_row)),
            dma((nk, 2, hops)), dma((nk, 2, hops)),
            dma((2, 2, hops)), dma((2, 2, hops)),
            dma((nk, NZ)), dma((2, nk, NZ)),
            dma((n_x - 1,)), dma((n_x - 1,)), dma((2,)),
        ]
        hbm = pl.BlockSpec(memory_space=pltpu.HBM)
        anywhere = pl.BlockSpec(memory_space=pl.ANY)
        results = pl.pallas_call(
            functools.partial(kernel, n_row, n_x, n_zh, T * n_dp),
            out_shape=(
                jax.ShapeDtypeStruct((3, 8, width), bf16),
                jax.ShapeDtypeStruct((3, 8, DR), bf16),
                jax.ShapeDtypeStruct((own, width), bf16),
                jax.ShapeDtypeStruct((own, width), f32),
                jax.ShapeDtypeStruct((own, width), f32),
            ),
            in_specs=[hbm] * 6,
            out_specs=(anywhere,) * 5,
            scratch_shapes=scratch,
            compiler_params=pltpu.CompilerParams(
                collective_id=0, has_side_effects=True, vmem_limit_bytes=48 * 1024 * 1024
            ),
        )(*(pltpu.with_memory_space_constraint(a, pltpu.HBM) for a in (inputs, weight, tall, anchor, first_moment, second_moment)))
        return write_out(results[0].reshape(24, width), results[1].reshape(24, DR), *results[2:])

    return per_device


def solution(mesh):
    in_specs = (
        P("dp", "row"),
        P("row", "col"),
        P(("dp", "row"), "col"),
        P(("row", "dp"), "col"),
        P(("row", "dp"), "col"),
        P(("row", "dp"), "col"),
    )
    out_specs = (
        P(("dp", "row"), "col"),
        P(("dp", "col"), "row"),
        P(("row", "dp"), "col"),
        P(("row", "dp"), "col"),
        P(("row", "dp"), "col"),
    )
    n_row, n_col = mesh.shape["row"], mesh.shape["col"]
    n_zh = 2 if n_col > 2 else 1
    return jax.shard_map(
        make_per_device(n_row, n_col // n_zh, n_zh), mesh=mesh,
        in_specs=in_specs, out_specs=out_specs, check_vma=False,
    )
```

```python
import functools

import jax
import jax.numpy as jnp
from jax import lax
from jax.experimental import pallas as pl
from jax.experimental.pallas import tpu as pltpu
from jax.sharding import PartitionSpec as P

beta_one = 0.9
beta_two = 0.999
learn_rate = 0.002
anchor_pull = 0.5
epsilon = 1e-08
step_count = 100.0

MESH = pl.DeviceIdType.MESH
f32, bf16 = jnp.float32, jnp.bfloat16
NZ = 4


def chunks_of(width):
    if width == 1792:
        sizes = (512, 384, 512, 384)
    else:
        sizes = (128,) * (width // 128)
    out, at = [], 0
    for size in sizes:
        out.append((at, size))
        at += size
    return out


def kernel(
    n_row, n_x, n_zh, tokens,
    x_ref, w_ref, ct_ref, an_ref, m_ref, v_ref,
    out_ref, ig_ref, nw_ref, nm_ref, nv_ref,
    xv, xpv, wv, ctb, ctp, xts, xs, xps, pb, rsr, gacc, gp, xr, zhs, zhr,
    zs, zr, acc, anv, mv, vv, outv, igv, nwv, nmv, nvv,
    load_sem, store_sem, x_sem, core_send, core_recv, ag_send, ag_recv, rs_send, rs_recv,
    z_send, z_recv, gx_send, gx_recv, zh_sem, token,
):
    width = w_ref.shape[1]
    T, DR = x_ref.shape
    blocks_of_rows = 2 * NZ
    own = DR // blocks_of_rows
    chunks = chunks_of(width)
    nk = len(chunks)
    dp, r, q = lax.axis_index("dp"), lax.axis_index("row"), lax.axis_index("col")
    z, c = dp // 2, dp % 2
    zh, xx = q // n_x, q % n_x
    right, left = lax.rem(r + 1, n_row), lax.rem(r + n_row - 1, n_row)
    ring = (right, left)
    sign = (1, -1)
    partner = 2 * z + (1 - c)

    def at_row(offset):
        return lax.rem(r + offset + 2 * n_row, n_row)

    def remote(src, dst, ssem, rsem, **device):
        return pltpu.make_async_remote_copy(
            src_ref=src, dst_ref=dst, send_sem=ssem, recv_sem=rsem,
            device_id=device, device_id_type=MESH,
        )

    def along_z(step):
        at = lax.rem(zh * NZ + z + step + NZ * n_zh, NZ * n_zh)
        return dict(dp=2 * lax.rem(at, NZ) + c, col=lax.div(at, NZ) * n_x + xx)

    def along_x(step):
        return dict(col=zh * n_x + lax.rem(xx + step + n_x, n_x))

    def signal(sem, device):
        pl.semaphore_signal(sem, inc=1, device_id=device, device_id_type=MESH)

    barrier = pltpu.get_barrier_semaphore()
    greet = [dict(row=right), dict(row=left), dict(dp=partner), along_z(1), along_z(-1)]
    greet += [along_x(1), along_x(-1)]
    if n_row > 4:
        greet += [dict(row=at_row(2)), dict(row=at_row(-2))]
    for device in greet:
        signal(barrier, device)

    loads = [
        pltpu.make_async_copy(x_ref, xv, load_sem.at[0]),
        pltpu.make_async_copy(w_ref, wv, load_sem.at[1]),
        pltpu.make_async_copy(ct_ref, ctb.at[r], load_sem.at[2]),
        pltpu.make_async_copy(m_ref, mv, load_sem.at[3]),
        pltpu.make_async_copy(v_ref, vv, load_sem.at[4]),
        pltpu.make_async_copy(an_ref, anv, load_sem.at[5]),
    ]
    for i in (2, 0, 1, 3, 4, 5):
        loads[i].start()

    def select(src, dst):
        xts[...] = src[...].T.reshape(NZ, 2, own, T)
        dst[...] = xts[:, c].reshape(NZ * own, T)

    loads[2].wait()
    pl.semaphore_wait(barrier, len(greet))

    sends = []

    def go(copy):
        copy.start()
        sends.append(copy)

    pieces = 2
    piece = width // pieces

    def steps_of(k, d):
        return n_row // 2 if (k + d) % 2 == 0 else (n_row - 1) // 2

    def ag_copy(k, d, reach, receiving):
        cols = pl.ds(k * piece, piece)
        hops = 1 if reach == 3 else min(reach, 2)
        block = at_row(-sign[d] * (reach if receiving else reach - hops))
        view = ctb.at[block, :, :, cols]
        return remote(
            view, view, ag_send.at[k, d, reach - 1], ag_recv.at[k, d, reach - 1],
            row=at_row(sign[d] * hops),
        )

    def core_copy(k, offset):
        cols = pl.ds(k * piece, piece)
        block = at_row(offset)
        slot = offset % n_row
        return remote(
            ctb.at[block, :, :, cols], ctp.at[block, :, :, cols],
            core_send.at[k, slot], core_recv.at[k, slot], dp=partner,
        )

    for reach in (2, 1):
        for k in range(pieces):
            for d in range(2):
                if reach <= steps_of(k, d):
                    go(ag_copy(k, d, reach, False))
    for k in range(pieces):
        go(core_copy(k, 0))
    if n_zh == 2:
        signal(token.at[0], along_z(1))
    if n_x > 2:
        signal(token.at[3], along_x(1))
    loads[0].wait()
    x_copy = remote(xv, xpv, x_sem.at[0], x_sem.at[1], dp=partner)
    go(x_copy)
    select(xv, xs)
    if n_zh == 2:
        pl.semaphore_wait(token.at[0], 1)
        signal(token.at[1], along_z(1))

    loads[1].wait()
    for at, size in chunks:
        part = jnp.dot(xv[...], wv[:, at:at + size], preferred_element_type=f32)
        pb[:, :, :, at:at + size] = part.reshape(n_row, 3, 8, size).astype(bf16)

    def gather(reach):
        for k in range(pieces):
            for d in range(2):
                if reach <= steps_of(k, d):
                    ag_copy(k, d, reach, True).wait_recv()
                    if reach == 2:
                        for further in (3, 4):
                            if further <= steps_of(k, d):
                                go(ag_copy(k, d, further, False))
                    go(core_copy(k, -sign[d] * reach))

    def rows_of(ref, at, size):
        return ref[:, :, :, at:at + size].astype(f32).reshape(T, size).astype(bf16)

    def multiply(k):
        at, size = chunks[k]
        mine = rows_of(ctb, at, size)
        other = rows_of(ctp, at, size)
        grad = jnp.dot(xs[...], mine, preferred_element_type=f32)
        grad = grad + jnp.dot(xps[...], other, preferred_element_type=f32)
        zs[:, :, at:at + size] = grad.reshape(NZ, own, size).astype(bf16)
        return mine

    def input_part(k, mine):
        at, size = chunks[k]
        part = lax.dot_general(
            mine, wv[:, at:at + size], (((1,), (1,)), ((), ())), preferred_element_type=f32
        )
        gacc[...] = part if k == 0 else gacc[...] + part

    def z_copy(k, way, d):
        cols = pl.ds(chunks[k][0], chunks[k][1])
        to = jnp.minimum(z + 1, NZ - 1) if way == 0 else jnp.maximum(z - 1, 0)
        return remote(
            zs.at[d, :, cols], zr.at[way, d, :, cols],
            z_send.at[k, d], z_recv.at[way, k, d], dp=2 * to + c,
        )

    def z_first(k, hops):
        for way, at_z, d in ((0, 0, hops), (1, NZ - 1, NZ - 1 - hops)):
            @pl.when(z == at_z)
            def _():
                z_copy(k, way, d).start()

    def z_relay(k, at_end, left):
        at, size = chunks[k]
        for way in range(2):
            here = at_end if way == 0 else NZ - 1 - at_end
            d = here + left if way == 0 else here - left

            @pl.when(z == here)
            def _():
                z_copy(k, way, d).wait_recv()
                both = zs[d, :, at:at + size].astype(f32) + zr[way, d, :, at:at + size].astype(f32)
                zs[d, :, at:at + size] = both.astype(bf16)
                z_copy(k, way, d).start()

    def z_wait_sends(k):
        for d in range(NZ):
            @pl.when(z != d)
            def _():
                z_copy(k, 0, d).wait_send()

    stores = []

    def put(src, dst, sem):
        copy = pltpu.make_async_copy(src, dst, sem)
        copy.start()
        stores.append(copy)

    def update(k):
        at, size = chunks[k]
        cols = pl.ds(at, size)
        acc[:, :size] = zs[z, :, at:at + size].astype(f32)
        for way, inner in ((0, z > 0), (1, z < NZ - 1)):
            @pl.when(inner)
            def _():
                z_copy(k, way, z).wait_recv()
                acc[:, :size] += zr[way, z, :, at:at + size].astype(f32)
        rows = pl.ds(pl.multiple_of(dp * own, own), own)
        current = wv[rows, at:at + size].astype(f32)
        grad = acc[:, :size] * (1.0 / tokens) + anchor_pull * (current - anv[:, at:at + size].astype(f32))
        first = beta_one * mv[:, at:at + size] + (1.0 - beta_one) * grad
        second = beta_two * vv[:, at:at + size] + (1.0 - beta_two) * grad * grad
        nmv[:, at:at + size] = first
        nvv[:, at:at + size] = second
        put(nmv.at[:, cols], nm_ref.at[:, cols], store_sem.at[k, 0])
        put(nvv.at[:, cols], nv_ref.at[:, cols], store_sem.at[k, 1])
        mhat = first * (1.0 / (1.0 - beta_one**step_count))
        vhat = second * (1.0 / (1.0 - beta_two**step_count))
        nwv[:, at:at + size] = (current - learn_rate * mhat / (jnp.sqrt(vhat) + epsilon)).astype(bf16)
        put(nwv.at[:, cols], nw_ref.at[:, cols], store_sem.at[k, 2])

    half = width // 2

    def rs_copy(h, d, step, receiving):
        total = steps_of(h, d)
        cols = pl.ds(h * half, half)
        target = at_row(sign[d] * (total - step - (1 if receiving else 0)))
        return remote(
            pb.at[target, :, :, cols], rsr.at[d, step, :, :, cols],
            rs_send.at[h, d, step], rs_recv.at[h, d, step], row=ring[d],
        )

    def rs_step(step):
        for h in range(2):
            for d in range(2):
                total = steps_of(h, d)
                cols = slice(h * half, (h + 1) * half)
                if step and step <= total:
                    rs_copy(h, d, step - 1, True).wait_recv()
                    if step < total:
                        block = at_row(sign[d] * (total - step))
                        both = pb[block, :, :, cols].astype(f32) + rsr[d, step - 1, :, :, cols].astype(f32)
                        pb[block, :, :, cols] = both.astype(bf16)
                if step < total:
                    go(rs_copy(h, d, step, False))

    def rs_finish():
        for h in range(2):
            cols = slice(h * half, (h + 1) * half)
            total = pb[r, :, :, cols].astype(f32)
            for d in range(2):
                if steps_of(h, d):
                    total = total + rsr[d, steps_of(h, d) - 1, :, :, cols].astype(f32)
            outv[:, :, cols] = total.astype(bf16)
        put(outv, out_ref, store_sem.at[nk, 0])

    def gx_copy(j):
        target = lax.rem(xx + j, n_x)
        return remote(
            gp.at[:, target], xr.at[j - 1], gx_send.at[j - 1], gx_recv.at[j - 1],
            col=zh * n_x + target,
        )

    def gx_start():
        gp[...] = gacc[...].reshape(n_zh, n_x, 3, 8, DR).astype(bf16)
        for j in range(1, n_x):
            go(gx_copy(j))

    def zh_copy():
        return remote(zhs, zhr, zh_sem.at[0], zh_sem.at[1], col=(1 - zh) * n_x + xx)

    def gx_finish():
        for j in range(1, n_x):
            gx_copy(j).wait_recv()

        def total(side):
            out = gp[side, xx].astype(f32)
            for j in range(1, n_x):
                out = out + xr[j - 1, side].astype(f32)
            return out

        if n_zh == 2:
            pl.semaphore_wait(token.at[2], 1)
            zhs[...] = total(1 - zh).astype(bf16)
            go(zh_copy())
        igv[...] = total(zh).astype(bf16)

    def ig_finish():
        if n_zh == 2:
            zh_copy().wait_recv()
            igv[...] = (igv[...].astype(f32) + zhr[...].astype(f32)).astype(bf16)
        put(igv, ig_ref, store_sem.at[nk, 1])

    hops = n_row // 2
    far = NZ - 1

    def finish_chunk(k):
        mine = multiply(k)
        z_first(k, far)
        input_part(k, mine)

    reaches = range(1, hops + 1)
    for reach in sorted(reaches, key=lambda n: abs(n - 2) + n / 8):
        gather(reach)
        if reach == min(2, hops):
            rs_step(0)
            x_copy.wait_recv()
            select(xpv, xps)
            if n_zh == 2:
                pl.semaphore_wait(token.at[1], 1)
                signal(token.at[2], along_z(1))
    for k in range(pieces):
        for slot in range(n_row):
            core_copy(k, slot).wait_recv()
        for m in range(nk):
            if k * piece <= chunks[m][0] < (k + 1) * piece:
                finish_chunk(m)
    if n_x > 2:
        pl.semaphore_wait(token.at[3], 1)
    gx_start()
    for k in range(nk):
        z_first(k, 2)
    rs_step(1)
    for k in range(nk + 1):
        if k < nk:
            z_relay(k, 1, 2)
        if k == 2:
            rs_step(2)
        if k:
            z_relay(k - 1, 2, 1)
    gx_finish()
    for k in range(nk):
        z_first(k, 1)
    rs_step(3)
    for k in range(nk):
        z_relay(k, 1, 1)
    for i in (3, 4, 5):
        loads[i].wait()
    for step in range(4, hops + 1):
        rs_step(step)
    rs_finish()
    ig_finish()
    for k in range(nk):
        update(k)

    for copy in sends:
        copy.wait_send()
    for k in range(nk):
        z_wait_sends(k)
    for copy in stores:
        copy.wait()


def write_kernel(*refs):
    n = (len(refs) - 1) // 2
    copies = [pltpu.make_async_copy(refs[i], refs[n + i], refs[-1].at[i]) for i in range(n)]
    for copy in copies:
        copy.start()
    for copy in copies:
        copy.wait()


def write_out(*arrays):
    n = len(arrays)
    return pl.pallas_call(
        write_kernel,
        out_shape=tuple(jax.ShapeDtypeStruct(a.shape, a.dtype) for a in arrays),
        in_specs=[pl.BlockSpec(memory_space=pl.ANY)] * n,
        out_specs=(pl.BlockSpec(memory_space=pltpu.HBM),) * n,
        scratch_shapes=[pltpu.SemaphoreType.DMA((n,))],
        compiler_params=pltpu.CompilerParams(vmem_limit_bytes=4 * 1024 * 1024),
    )(*arrays)


def make_per_device(n_row, n_x, n_zh, n_dp=8):
    def per_device(inputs, weight, cotangent, anchor, first_moment, second_moment):
        T, DR = inputs.shape
        width = weight.shape[1]
        own = DR // n_dp
        nk = len(chunks_of(width))
        hops = max(n_row // 2, 1)
        tall = cotangent.reshape(3, 8, width)
        dma = pltpu.SemaphoreType.DMA
        V = pltpu.VMEM
        scratch = [
            V((T, DR), bf16), V((T, DR), bf16), V((DR, width), bf16),
            V((n_row, 3, 8, width), bf16), V((n_row, 3, 8, width), bf16),
            V((NZ, 2, own, T), bf16), V((NZ * own, T), bf16), V((NZ * own, T), bf16),
            V((n_row, 3, 8, width), bf16), V((2, hops, 3, 8, width), bf16),
            V((T, DR), f32), V((n_zh, n_x, 3, 8, DR), bf16), V((n_x - 1, n_zh, 3, 8, DR), bf16),
            V((3, 8, DR), bf16), V((3, 8, DR), bf16),
            V((NZ, own, width), bf16), V((2, NZ, own, width), bf16), V((own, 512), f32),
            V((own, width), bf16), V((own, width), f32), V((own, width), f32),
            V((3, 8, width), bf16), V((3, 8, DR), bf16),
            V((own, width), bf16), V((own, width), f32), V((own, width), f32),
            dma((6,)), dma((nk + 1, 3)), dma((2,)),
            dma((2, n_row)), dma((2, n_row)),
            dma((2, 2, hops)), dma((2, 2, hops)),
            dma((2, 2, hops)), dma((2, 2, hops)),
            dma((nk, NZ)), dma((2, nk, NZ)),
            dma((n_x - 1,)), dma((n_x - 1,)), dma((2,)),
            pltpu.SemaphoreType.REGULAR((4,)),
        ]
        hbm = pl.BlockSpec(memory_space=pltpu.HBM)
        anywhere = pl.BlockSpec(memory_space=pl.ANY)
        results = pl.pallas_call(
            functools.partial(kernel, n_row, n_x, n_zh, T * n_dp),
            out_shape=(
                jax.ShapeDtypeStruct((3, 8, width), bf16),
                jax.ShapeDtypeStruct((3, 8, DR), bf16),
                jax.ShapeDtypeStruct((own, width), bf16),
                jax.ShapeDtypeStruct((own, width), f32),
                jax.ShapeDtypeStruct((own, width), f32),
            ),
            in_specs=[hbm] * 6,
            out_specs=(anywhere,) * 5,
            scratch_shapes=scratch,
            compiler_params=pltpu.CompilerParams(
                collective_id=0, has_side_effects=True, vmem_limit_bytes=48 * 1024 * 1024
            ),
        )(*(pltpu.with_memory_space_constraint(a, pltpu.HBM) for a in (inputs, weight, tall, anchor, first_moment, second_moment)))
        return write_out(results[0].reshape(24, width), results[1].reshape(24, DR), *results[2:])

    return per_device


def solution(mesh):
    in_specs = (
        P("dp", "row"),
        P("row", "col"),
        P(("dp", "row"), "col"),
        P(("row", "dp"), "col"),
        P(("row", "dp"), "col"),
        P(("row", "dp"), "col"),
    )
    out_specs = (
        P(("dp", "row"), "col"),
        P(("dp", "col"), "row"),
        P(("row", "dp"), "col"),
        P(("row", "dp"), "col"),
        P(("row", "dp"), "col"),
    )
    n_row, n_col = mesh.shape["row"], mesh.shape["col"]
    n_zh = 2 if n_col > 2 else 1
    return jax.shard_map(
        make_per_device(n_row, n_col // n_zh, n_zh), mesh=mesh,
        in_specs=in_specs, out_specs=out_specs, check_vma=False,
    )
```

```python
import functools

import jax
import jax.numpy as jnp
from jax import lax
from jax.experimental import pallas as pl
from jax.experimental.pallas import tpu as pltpu
from jax.sharding import PartitionSpec as P

beta_one = 0.9
beta_two = 0.999
learn_rate = 0.002
anchor_pull = 0.5
epsilon = 1e-08
step_count = 100.0

MESH = pl.DeviceIdType.MESH
f32, bf16 = jnp.float32, jnp.bfloat16
NZ = 4


def chunks_of(width):
    if width == 1792:
        sizes = (256, 512, 512, 512)
    else:
        sizes = (128,) * (width // 128)
    out, at = [], 0
    for size in sizes:
        out.append((at, size))
        at += size
    return out


def kernel(
    n_row, n_x, n_zh, tokens,
    x_ref, w_ref, ct_ref, an_ref, m_ref, v_ref,
    out_ref, ig_ref, nw_ref, nm_ref, nv_ref,
    xv, xpv, wv, ctb, ctp, xts, xs, xps, wacc, pb, rsr, gacc, gp, xr, zhs, zhr,
    zs, zr, acc, anv, mv, vv, outv, igv, nwv, nmv, nvv,
    load_sem, store_sem, x_sem, core_send, core_recv, ag_send, ag_recv, rs_send, rs_recv,
    z_send, z_recv, gx_send, gx_recv, zh_sem, token,
):
    width = w_ref.shape[1]
    T, DR = x_ref.shape
    blocks_of_rows = 2 * NZ
    own = DR // blocks_of_rows
    chunks = chunks_of(width)
    nk = len(chunks)
    dp, r, q = lax.axis_index("dp"), lax.axis_index("row"), lax.axis_index("col")
    z, c = dp // 2, dp % 2
    zh, xx = q // n_x, q % n_x
    right, left = lax.rem(r + 1, n_row), lax.rem(r + n_row - 1, n_row)
    ring = (right, left)
    sign = (1, -1)
    partner = 2 * z + (1 - c)

    def at_row(offset):
        return lax.rem(r + offset + 2 * n_row, n_row)

    def remote(src, dst, ssem, rsem, **device):
        return pltpu.make_async_remote_copy(
            src_ref=src, dst_ref=dst, send_sem=ssem, recv_sem=rsem,
            device_id=device, device_id_type=MESH,
        )

    def along_z(step):
        at = lax.rem(zh * NZ + z + step + NZ * n_zh, NZ * n_zh)
        return dict(dp=2 * lax.rem(at, NZ) + c, col=lax.div(at, NZ) * n_x + xx)

    def along_x(step):
        return dict(col=zh * n_x + lax.rem(xx + step + n_x, n_x))

    def signal(sem, device):
        pl.semaphore_signal(sem, inc=1, device_id=device, device_id_type=MESH)

    barrier = pltpu.get_barrier_semaphore()
    greet = [dict(row=right), dict(row=left), dict(dp=partner), along_z(1), along_z(-1)]
    greet += [along_x(1), along_x(-1)]
    if n_row > 4:
        greet += [dict(row=at_row(2)), dict(row=at_row(-2))]
    for device in greet:
        signal(barrier, device)

    loads = [
        pltpu.make_async_copy(x_ref, xv, load_sem.at[0]),
        pltpu.make_async_copy(w_ref, wv, load_sem.at[1]),
        pltpu.make_async_copy(ct_ref, ctb.at[r], load_sem.at[2]),
        pltpu.make_async_copy(m_ref, mv, load_sem.at[3]),
        pltpu.make_async_copy(v_ref, vv, load_sem.at[4]),
        pltpu.make_async_copy(an_ref, anv, load_sem.at[5]),
    ]
    for i in (2, 0, 1, 3, 4, 5):
        loads[i].start()

    def select(src, dst):
        xts[...] = src[...].T.reshape(NZ, 2, own, T)
        dst[...] = xts[:, c].reshape(NZ * own, T)

    loads[2].wait()
    pl.semaphore_wait(barrier, len(greet))

    sends = []

    def go(copy):
        copy.start()
        sends.append(copy)

    def steps_of(k, d):
        return n_row // 2 if (k + d) % 2 == 0 else (n_row - 1) // 2

    def ag_copy(k, d, reach, receiving):
        cols = pl.ds(chunks[k][0], chunks[k][1])
        hops = 1 if reach == 3 else min(reach, 2)
        block = at_row(-sign[d] * (reach if receiving else reach - hops))
        view = ctb.at[block, :, :, cols]
        return remote(
            view, view, ag_send.at[k, d, reach - 1], ag_recv.at[k, d, reach - 1],
            row=at_row(sign[d] * hops),
        )

    def core_copy(k, offset):
        cols = pl.ds(chunks[k][0], chunks[k][1])
        block = at_row(offset)
        slot = offset % n_row
        return remote(
            ctb.at[block, :, :, cols], ctp.at[block, :, :, cols],
            core_send.at[k, slot], core_recv.at[k, slot], dp=partner,
        )

    for k in range(nk):
        for reach in (2, 1):
            for d in range(2):
                if reach <= steps_of(k, d):
                    go(ag_copy(k, d, reach, False))
    for k in range(nk):
        go(core_copy(k, 0))
    if n_zh == 2:
        signal(token.at[0], along_z(1))
    if n_x > 2:
        signal(token.at[3], along_x(1))
    loads[0].wait()
    x_copy = remote(xv, xpv, x_sem.at[0], x_sem.at[1], dp=partner)
    go(x_copy)
    select(xv, xs)
    if n_zh == 2:
        pl.semaphore_wait(token.at[0], 1)
        signal(token.at[1], along_z(1))

    loads[1].wait()
    for at, size in chunks:
        part = jnp.dot(xv[...], wv[:, at:at + size], preferred_element_type=f32)
        pb[:, :, :, at:at + size] = part.reshape(n_row, 3, 8, size).astype(bf16)

    def gather(k, reach):
        for d in range(2):
            if reach <= steps_of(k, d):
                ag_copy(k, d, reach, True).wait_recv()
                if reach == 2:
                    for further in (3, 4):
                        if further <= steps_of(k, d):
                            go(ag_copy(k, d, further, False))
                go(core_copy(k, -sign[d] * reach))

    def rows_of(ref, at, size):
        return ref[:, :, :, at:at + size].astype(f32).reshape(T, size).astype(bf16)

    def own_part(k):
        at, size = chunks[k]
        mine = rows_of(ctb, at, size)
        wacc[:, at:at + size] = jnp.dot(xs[...], mine, preferred_element_type=f32)
        part = lax.dot_general(
            mine, wv[:, at:at + size], (((1,), (1,)), ((), ())), preferred_element_type=f32
        )
        gacc[...] = part if k == 0 else gacc[...] + part

    def other_part(k):
        at, size = chunks[k]
        other = rows_of(ctp, at, size)
        grad = wacc[:, at:at + size] + jnp.dot(xps[...], other, preferred_element_type=f32)
        zs[:, :, at:at + size] = grad.reshape(NZ, own, size).astype(bf16)

    def z_copy(k, way, d):
        cols = pl.ds(chunks[k][0], chunks[k][1])
        to = jnp.minimum(z + 1, NZ - 1) if way == 0 else jnp.maximum(z - 1, 0)
        return remote(
            zs.at[d, :, cols], zr.at[way, d, :, cols],
            z_send.at[k, d], z_recv.at[way, k, d], dp=2 * to + c,
        )

    def z_first(k, hops):
        for way, at_z, d in ((0, 0, hops), (1, NZ - 1, NZ - 1 - hops)):
            @pl.when(z == at_z)
            def _():
                z_copy(k, way, d).start()

    def z_relay(k, at_end, left):
        at, size = chunks[k]
        for way in range(2):
            here = at_end if way == 0 else NZ - 1 - at_end
            d = here + left if way == 0 else here - left

            @pl.when(z == here)
            def _():
                z_copy(k, way, d).wait_recv()
                both = zs[d, :, at:at + size].astype(f32) + zr[way, d, :, at:at + size].astype(f32)
                zs[d, :, at:at + size] = both.astype(bf16)
                z_copy(k, way, d).start()

    def z_wait_sends(k):
        for d in range(NZ):
            @pl.when(z != d)
            def _():
                z_copy(k, 0, d).wait_send()

    stores = []

    def put(src, dst, sem):
        copy = pltpu.make_async_copy(src, dst, sem)
        copy.start()
        stores.append(copy)

    def update(k):
        at, size = chunks[k]
        cols = pl.ds(at, size)
        acc[:, :size] = zs[z, :, at:at + size].astype(f32)
        for way, inner in ((0, z > 0), (1, z < NZ - 1)):
            @pl.when(inner)
            def _():
                z_copy(k, way, z).wait_recv()
                acc[:, :size] += zr[way, z, :, at:at + size].astype(f32)
        rows = pl.ds(pl.multiple_of(dp * own, own), own)
        current = wv[rows, at:at + size].astype(f32)
        grad = acc[:, :size] * (1.0 / tokens) + anchor_pull * (current - anv[:, at:at + size].astype(f32))
        first = beta_one * mv[:, at:at + size] + (1.0 - beta_one) * grad
        second = beta_two * vv[:, at:at + size] + (1.0 - beta_two) * grad * grad
        nmv[:, at:at + size] = first
        nvv[:, at:at + size] = second
        put(nmv.at[:, cols], nm_ref.at[:, cols], store_sem.at[k, 0])
        put(nvv.at[:, cols], nv_ref.at[:, cols], store_sem.at[k, 1])
        mhat = first * (1.0 / (1.0 - beta_one**step_count))
        vhat = second * (1.0 / (1.0 - beta_two**step_count))
        nwv[:, at:at + size] = (current - learn_rate * mhat / (jnp.sqrt(vhat) + epsilon)).astype(bf16)
        put(nwv.at[:, cols], nw_ref.at[:, cols], store_sem.at[k, 2])

    half = width // 2

    def rs_copy(h, d, step, receiving):
        total = steps_of(h, d)
        cols = pl.ds(h * half, half)
        target = at_row(sign[d] * (total - step - (1 if receiving else 0)))
        return remote(
            pb.at[target, :, :, cols], rsr.at[d, step, :, :, cols],
            rs_send.at[h, d, step], rs_recv.at[h, d, step], row=ring[d],
        )

    def rs_step(step):
        for h in range(2):
            for d in range(2):
                total = steps_of(h, d)
                cols = slice(h * half, (h + 1) * half)
                if step and step <= total:
                    rs_copy(h, d, step - 1, True).wait_recv()
                    if step < total:
                        block = at_row(sign[d] * (total - step))
                        both = pb[block, :, :, cols].astype(f32) + rsr[d, step - 1, :, :, cols].astype(f32)
                        pb[block, :, :, cols] = both.astype(bf16)
                if step < total:
                    go(rs_copy(h, d, step, False))

    def rs_finish():
        for h in range(2):
            cols = slice(h * half, (h + 1) * half)
            total = pb[r, :, :, cols].astype(f32)
            for d in range(2):
                if steps_of(h, d):
                    total = total + rsr[d, steps_of(h, d) - 1, :, :, cols].astype(f32)
            outv[:, :, cols] = total.astype(bf16)
        put(outv, out_ref, store_sem.at[nk, 0])

    def gx_copy(j):
        target = lax.rem(xx + j, n_x)
        return remote(
            gp.at[:, target], xr.at[j - 1], gx_send.at[j - 1], gx_recv.at[j - 1],
            col=zh * n_x + target,
        )

    def gx_start():
        gp[...] = gacc[...].reshape(n_zh, n_x, 3, 8, DR).astype(bf16)
        for j in range(1, n_x):
            go(gx_copy(j))

    def zh_copy():
        return remote(zhs, zhr, zh_sem.at[0], zh_sem.at[1], col=(1 - zh) * n_x + xx)

    def gx_finish():
        for j in range(1, n_x):
            gx_copy(j).wait_recv()

        def total(side):
            out = gp[side, xx].astype(f32)
            for j in range(1, n_x):
                out = out + xr[j - 1, side].astype(f32)
            return out

        if n_zh == 2:
            pl.semaphore_wait(token.at[2], 1)
            zhs[...] = total(1 - zh).astype(bf16)
            go(zh_copy())
        igv[...] = total(zh).astype(bf16)

    def ig_finish():
        if n_zh == 2:
            zh_copy().wait_recv()
            igv[...] = (igv[...].astype(f32) + zhr[...].astype(f32)).astype(bf16)
        put(igv, ig_ref, store_sem.at[nk, 1])

    hops = n_row // 2
    far = NZ - 1

    def finish_chunk(k):
        for slot in range(n_row):
            core_copy(k, slot).wait_recv()
        other_part(k)
        z_first(k, far)

    for k in range(nk):
        gather(k, 2)
    rs_step(0)
    x_copy.wait_recv()
    select(xpv, xps)
    if n_zh == 2:
        pl.semaphore_wait(token.at[1], 1)
        signal(token.at[2], along_z(1))
    for k in range(nk):
        for reach in range(1, hops + 1):
            if reach != 2:
                gather(k, reach)
        if k:
            finish_chunk(k - 1)
        own_part(k)
    if n_x > 2:
        pl.semaphore_wait(token.at[3], 1)
    gx_start()
    rs_step(1)
    finish_chunk(nk - 1)
    for k in range(nk):
        z_first(k, 2)
    for k in range(nk + 1):
        if k < nk:
            z_relay(k, 1, 2)
        if k == 0:
            rs_step(2)
        if k == 1:
            gx_finish()
        if k == 3:
            rs_step(3)
        if k:
            z_relay(k - 1, 2, 1)
    for k in range(nk):
        z_first(k, 1)
    for k in range(nk):
        z_relay(k, 1, 1)
    for i in (3, 4, 5):
        loads[i].wait()
    for step in range(4, hops + 1):
        rs_step(step)
    rs_finish()
    ig_finish()
    for k in range(nk):
        update(k)

    for copy in sends:
        copy.wait_send()
    for k in range(nk):
        z_wait_sends(k)
    for copy in stores:
        copy.wait()


def write_kernel(*refs):
    n = (len(refs) - 1) // 2
    copies = [pltpu.make_async_copy(refs[i], refs[n + i], refs[-1].at[i]) for i in range(n)]
    for copy in copies:
        copy.start()
    for copy in copies:
        copy.wait()


def write_out(*arrays):
    n = len(arrays)
    return pl.pallas_call(
        write_kernel,
        out_shape=tuple(jax.ShapeDtypeStruct(a.shape, a.dtype) for a in arrays),
        in_specs=[pl.BlockSpec(memory_space=pl.ANY)] * n,
        out_specs=(pl.BlockSpec(memory_space=pltpu.HBM),) * n,
        scratch_shapes=[pltpu.SemaphoreType.DMA((n,))],
        compiler_params=pltpu.CompilerParams(vmem_limit_bytes=4 * 1024 * 1024),
    )(*arrays)


def make_per_device(n_row, n_x, n_zh, n_dp=8):
    def per_device(inputs, weight, cotangent, anchor, first_moment, second_moment):
        T, DR = inputs.shape
        width = weight.shape[1]
        own = DR // n_dp
        nk = len(chunks_of(width))
        hops = max(n_row // 2, 1)
        tall = cotangent.reshape(3, 8, width)
        dma = pltpu.SemaphoreType.DMA
        V = pltpu.VMEM
        scratch = [
            V((T, DR), bf16), V((T, DR), bf16), V((DR, width), bf16),
            V((n_row, 3, 8, width), bf16), V((n_row, 3, 8, width), bf16),
            V((NZ, 2, own, T), bf16), V((NZ * own, T), bf16), V((NZ * own, T), bf16),
            V((NZ * own, width), f32),
            V((n_row, 3, 8, width), bf16), V((2, hops, 3, 8, width), bf16),
            V((T, DR), f32), V((n_zh, n_x, 3, 8, DR), bf16), V((n_x - 1, n_zh, 3, 8, DR), bf16),
            V((3, 8, DR), bf16), V((3, 8, DR), bf16),
            V((NZ, own, width), bf16), V((2, NZ, own, width), bf16), V((own, 512), f32),
            V((own, width), bf16), V((own, width), f32), V((own, width), f32),
            V((3, 8, width), bf16), V((3, 8, DR), bf16),
            V((own, width), bf16), V((own, width), f32), V((own, width), f32),
            dma((6,)), dma((nk + 1, 3)), dma((2,)),
            dma((nk, n_row)), dma((nk, n_row)),
            dma((nk, 2, hops)), dma((nk, 2, hops)),
            dma((2, 2, hops)), dma((2, 2, hops)),
            dma((nk, NZ)), dma((2, nk, NZ)),
            dma((n_x - 1,)), dma((n_x - 1,)), dma((2,)),
            pltpu.SemaphoreType.REGULAR((4,)),
        ]
        hbm = pl.BlockSpec(memory_space=pltpu.HBM)
        anywhere = pl.BlockSpec(memory_space=pl.ANY)
        results = pl.pallas_call(
            functools.partial(kernel, n_row, n_x, n_zh, T * n_dp),
            out_shape=(
                jax.ShapeDtypeStruct((3, 8, width), bf16),
                jax.ShapeDtypeStruct((3, 8, DR), bf16),
                jax.ShapeDtypeStruct((own, width), bf16),
                jax.ShapeDtypeStruct((own, width), f32),
                jax.ShapeDtypeStruct((own, width), f32),
            ),
            in_specs=[hbm] * 6,
            out_specs=(anywhere,) * 5,
            scratch_shapes=scratch,
            compiler_params=pltpu.CompilerParams(
                collective_id=0, has_side_effects=True, vmem_limit_bytes=48 * 1024 * 1024
            ),
        )(*(pltpu.with_memory_space_constraint(a, pltpu.HBM) for a in (inputs, weight, tall, anchor, first_moment, second_moment)))
        return write_out(results[0].reshape(24, width), results[1].reshape(24, DR), *results[2:])

    return per_device


def solution(mesh):
    in_specs = (
        P("dp", "row"),
        P("row", "col"),
        P(("dp", "row"), "col"),
        P(("row", "dp"), "col"),
        P(("row", "dp"), "col"),
        P(("row", "dp"), "col"),
    )
    out_specs = (
        P(("dp", "row"), "col"),
        P(("dp", "col"), "row"),
        P(("row", "dp"), "col"),
        P(("row", "dp"), "col"),
        P(("row", "dp"), "col"),
    )
    n_row, n_col = mesh.shape["row"], mesh.shape["col"]
    n_zh = 2 if n_col > 2 else 1
    return jax.shard_map(
        make_per_device(n_row, n_col // n_zh, n_zh), mesh=mesh,
        in_specs=in_specs, out_specs=out_specs, check_vma=False,
    )
```

```python
import functools

import jax
import jax.numpy as jnp
from jax import lax
from jax.experimental import pallas as pl
from jax.experimental.pallas import tpu as pltpu
from jax.sharding import PartitionSpec as P

beta_one = 0.9
beta_two = 0.999
learn_rate = 0.002
anchor_pull = 0.5
epsilon = 1e-08
step_count = 100.0

MESH = pl.DeviceIdType.MESH
f32, bf16 = jnp.float32, jnp.bfloat16
NZ = 4


def chunks_of(width):
    if width == 1792:
        sizes = (256, 512, 512, 512)
    else:
        sizes = (128,) * (width // 128)
    out, at = [], 0
    for size in sizes:
        out.append((at, size))
        at += size
    return out


def kernel(
    n_row, n_x, n_zh, tokens,
    x_ref, w_ref, ct_ref, an_ref, m_ref, v_ref,
    outv, igv, nwv, nmv, nvv,
    xv, xpv, wv, ctb, ctp, xts, xs, xps, wacc, pb, rsr, gacc, gp, xr, zhs, zhr,
    zs, zr, acc, anv, mv, vv,
    load_sem, x_sem, core_send, core_recv, ag_send, ag_recv, rs_send, rs_recv,
    z_send, z_recv, gx_send, gx_recv, zh_sem, token,
):
    width = w_ref.shape[1]
    T, DR = x_ref.shape
    blocks_of_rows = 2 * NZ
    own = DR // blocks_of_rows
    chunks = chunks_of(width)
    nk = len(chunks)
    dp, r, q = lax.axis_index("dp"), lax.axis_index("row"), lax.axis_index("col")
    z, c = dp // 2, dp % 2
    zh, xx = q // n_x, q % n_x
    right, left = lax.rem(r + 1, n_row), lax.rem(r + n_row - 1, n_row)
    ring = (right, left)
    sign = (1, -1)
    partner = 2 * z + (1 - c)

    def at_row(offset):
        return lax.rem(r + offset + 2 * n_row, n_row)

    def remote(src, dst, ssem, rsem, **device):
        return pltpu.make_async_remote_copy(
            src_ref=src, dst_ref=dst, send_sem=ssem, recv_sem=rsem,
            device_id=device, device_id_type=MESH,
        )

    def along_z(step):
        at = lax.rem(zh * NZ + z + step + NZ * n_zh, NZ * n_zh)
        return dict(dp=2 * lax.rem(at, NZ) + c, col=lax.div(at, NZ) * n_x + xx)

    def along_x(step):
        return dict(col=zh * n_x + lax.rem(xx + step + n_x, n_x))

    def signal(sem, device):
        pl.semaphore_signal(sem, inc=1, device_id=device, device_id_type=MESH)

    barrier = pltpu.get_barrier_semaphore()
    greet = [dict(row=right), dict(row=left), dict(dp=partner), along_z(1), along_z(-1)]
    greet += [along_x(1), along_x(-1)]
    if n_row > 4:
        greet += [dict(row=at_row(2)), dict(row=at_row(-2))]
    for device in greet:
        signal(barrier, device)

    loads = [
        pltpu.make_async_copy(x_ref, xv, load_sem.at[0]),
        pltpu.make_async_copy(w_ref, wv, load_sem.at[1]),
        pltpu.make_async_copy(ct_ref, ctb.at[r], load_sem.at[2]),
        pltpu.make_async_copy(m_ref, mv, load_sem.at[3]),
        pltpu.make_async_copy(v_ref, vv, load_sem.at[4]),
        pltpu.make_async_copy(an_ref, anv, load_sem.at[5]),
    ]
    for i in (2, 0, 1, 3, 4, 5):
        loads[i].start()

    def select(src, dst):
        xts[...] = src[...].T.reshape(NZ, 2, own, T)
        dst[...] = xts[:, c].reshape(NZ * own, T)

    loads[2].wait()
    pl.semaphore_wait(barrier, len(greet))

    sends = []

    def go(copy):
        copy.start()
        sends.append(copy)

    def steps_of(k, d):
        return n_row // 2 if (k + d) % 2 == 0 else (n_row - 1) // 2

    def ag_copy(k, d, reach, receiving):
        cols = pl.ds(chunks[k][0], chunks[k][1])
        hops = 1 if reach == 3 else min(reach, 2)
        block = at_row(-sign[d] * (reach if receiving else reach - hops))
        view = ctb.at[block, :, :, cols]
        return remote(
            view, view, ag_send.at[k, d, reach - 1], ag_recv.at[k, d, reach - 1],
            row=at_row(sign[d] * hops),
        )

    def core_copy(k, offset):
        cols = pl.ds(chunks[k][0], chunks[k][1])
        block = at_row(offset)
        slot = offset % n_row
        return remote(
            ctb.at[block, :, :, cols], ctp.at[block, :, :, cols],
            core_send.at[k, slot], core_recv.at[k, slot], dp=partner,
        )

    for k in range(nk):
        for reach in (2, 1):
            for d in range(2):
                if reach <= steps_of(k, d):
                    go(ag_copy(k, d, reach, False))
    for k in range(nk):
        go(core_copy(k, 0))
    if n_zh == 2:
        signal(token.at[0], along_z(1))
    if n_x > 2:
        signal(token.at[3], along_x(1))
    loads[0].wait()
    x_copy = remote(xv, xpv, x_sem.at[0], x_sem.at[1], dp=partner)
    go(x_copy)
    select(xv, xs)
    if n_zh == 2:
        pl.semaphore_wait(token.at[0], 1)
        signal(token.at[1], along_z(1))

    loads[1].wait()
    for at, size in chunks:
        part = jnp.dot(xv[...], wv[:, at:at + size], preferred_element_type=f32)
        pb[:, :, :, at:at + size] = part.reshape(n_row, 3, 8, size).astype(bf16)

    def gather(k, reach):
        for d in range(2):
            if reach <= steps_of(k, d):
                ag_copy(k, d, reach, True).wait_recv()
                if reach == 2:
                    for further in (3, 4):
                        if further <= steps_of(k, d):
                            go(ag_copy(k, d, further, False))
                go(core_copy(k, -sign[d] * reach))

    def rows_of(ref, at, size):
        return ref[:, :, :, at:at + size].astype(f32).reshape(T, size).astype(bf16)

    def own_part(k):
        at, size = chunks[k]
        mine = rows_of(ctb, at, size)
        wacc[:, at:at + size] = jnp.dot(xs[...], mine, preferred_element_type=f32)
        part = lax.dot_general(
            mine, wv[:, at:at + size], (((1,), (1,)), ((), ())), preferred_element_type=f32
        )
        gacc[...] = part if k == 0 else gacc[...] + part

    def other_part(k):
        at, size = chunks[k]
        other = rows_of(ctp, at, size)
        grad = wacc[:, at:at + size] + jnp.dot(xps[...], other, preferred_element_type=f32)
        zs[:, :, at:at + size] = grad.reshape(NZ, own, size).astype(bf16)

    def z_copy(k, way, d):
        cols = pl.ds(chunks[k][0], chunks[k][1])
        to = jnp.minimum(z + 1, NZ - 1) if way == 0 else jnp.maximum(z - 1, 0)
        return remote(
            zs.at[d, :, cols], zr.at[way, d, :, cols],
            z_send.at[k, d], z_recv.at[way, k, d], dp=2 * to + c,
        )

    def z_first(k, hops):
        for way, at_z, d in ((0, 0, hops), (1, NZ - 1, NZ - 1 - hops)):
            @pl.when(z == at_z)
            def _():
                z_copy(k, way, d).start()

    def z_relay(k, at_end, left):
        at, size = chunks[k]
        for way in range(2):
            here = at_end if way == 0 else NZ - 1 - at_end
            d = here + left if way == 0 else here - left

            @pl.when(z == here)
            def _():
                z_copy(k, way, d).wait_recv()
                both = zs[d, :, at:at + size].astype(f32) + zr[way, d, :, at:at + size].astype(f32)
                zs[d, :, at:at + size] = both.astype(bf16)
                z_copy(k, way, d).start()

    def z_wait_sends(k):
        for d in range(NZ):
            @pl.when(z != d)
            def _():
                z_copy(k, 0, d).wait_send()

    def update(k):
        at, size = chunks[k]
        acc[:, :size] = zs[z, :, at:at + size].astype(f32)
        for way, inner in ((0, z > 0), (1, z < NZ - 1)):
            @pl.when(inner)
            def _():
                z_copy(k, way, z).wait_recv()
                acc[:, :size] += zr[way, z, :, at:at + size].astype(f32)
        rows = pl.ds(pl.multiple_of(dp * own, own), own)
        current = wv[rows, at:at + size].astype(f32)
        grad = acc[:, :size] * (1.0 / tokens) + anchor_pull * (current - anv[:, at:at + size].astype(f32))
        first = beta_one * mv[:, at:at + size] + (1.0 - beta_one) * grad
        second = beta_two * vv[:, at:at + size] + (1.0 - beta_two) * grad * grad
        nmv[:, at:at + size] = first
        nvv[:, at:at + size] = second
        mhat = first * (1.0 / (1.0 - beta_one**step_count))
        vhat = second * (1.0 / (1.0 - beta_two**step_count))
        nwv[:, at:at + size] = (current - learn_rate * mhat / (jnp.sqrt(vhat) + epsilon)).astype(bf16)

    half = width // 2

    def rs_copy(h, d, step, receiving):
        total = steps_of(h, d)
        cols = pl.ds(h * half, half)
        target = at_row(sign[d] * (total - step - (1 if receiving else 0)))
        return remote(
            pb.at[target, :, :, cols], rsr.at[d, step, :, :, cols],
            rs_send.at[h, d, step], rs_recv.at[h, d, step], row=ring[d],
        )

    def rs_step(step):
        for h in range(2):
            for d in range(2):
                total = steps_of(h, d)
                cols = slice(h * half, (h + 1) * half)
                if step and step <= total:
                    rs_copy(h, d, step - 1, True).wait_recv()
                    if step < total:
                        block = at_row(sign[d] * (total - step))
                        both = pb[block, :, :, cols].astype(f32) + rsr[d, step - 1, :, :, cols].astype(f32)
                        pb[block, :, :, cols] = both.astype(bf16)
                if step < total:
                    go(rs_copy(h, d, step, False))

    def rs_finish():
        for h in range(2):
            cols = slice(h * half, (h + 1) * half)
            total = pb[r, :, :, cols].astype(f32)
            for d in range(2):
                if steps_of(h, d):
                    total = total + rsr[d, steps_of(h, d) - 1, :, :, cols].astype(f32)
            outv[:, :, cols] = total.astype(bf16)

    def gx_copy(j):
        target = lax.rem(xx + j, n_x)
        return remote(
            gp.at[:, target], xr.at[j - 1], gx_send.at[j - 1], gx_recv.at[j - 1],
            col=zh * n_x + target,
        )

    def gx_start():
        gp[...] = gacc[...].reshape(n_zh, n_x, 3, 8, DR).astype(bf16)
        for j in range(1, n_x):
            go(gx_copy(j))

    def zh_copy():
        return remote(zhs, zhr, zh_sem.at[0], zh_sem.at[1], col=(1 - zh) * n_x + xx)

    def gx_finish():
        for j in range(1, n_x):
            gx_copy(j).wait_recv()

        def total(side):
            out = gp[side, xx].astype(f32)
            for j in range(1, n_x):
                out = out + xr[j - 1, side].astype(f32)
            return out

        if n_zh == 2:
            pl.semaphore_wait(token.at[2], 1)
            zhs[...] = total(1 - zh).astype(bf16)
            go(zh_copy())
        igv[...] = total(zh).astype(bf16)

    def ig_finish():
        if n_zh == 2:
            zh_copy().wait_recv()
            igv[...] = (igv[...].astype(f32) + zhr[...].astype(f32)).astype(bf16)

    hops = n_row // 2
    far = NZ - 1

    def finish_chunk(k):
        for slot in range(n_row):
            core_copy(k, slot).wait_recv()
        other_part(k)
        z_first(k, far)

    for k in range(nk):
        gather(k, 2)
    rs_step(0)
    x_copy.wait_recv()
    select(xpv, xps)
    if n_zh == 2:
        pl.semaphore_wait(token.at[1], 1)
        signal(token.at[2], along_z(1))
    for k in range(nk):
        for reach in range(1, hops + 1):
            if reach != 2:
                gather(k, reach)
        if k == nk - 1:
            rs_step(1)
        if k:
            finish_chunk(k - 1)
        own_part(k)
    if n_x > 2:
        pl.semaphore_wait(token.at[3], 1)
    gx_start()
    finish_chunk(nk - 1)
    for k in range(nk):
        z_first(k, 2)
    for k in range(nk + 1):
        if k < nk:
            z_relay(k, 1, 2)
        if k == 0:
            rs_step(2)
        if k == 1:
            gx_finish()
        if k == 2:
            rs_step(3)
        if k:
            z_relay(k - 1, 2, 1)
    for k in range(nk):
        z_first(k, 1)
    for k in range(nk):
        z_relay(k, 1, 1)
    for i in (3, 4, 5):
        loads[i].wait()
    for step in range(4, hops + 1):
        rs_step(step)
    rs_finish()
    ig_finish()
    for k in range(nk):
        update(k)

    for copy in sends:
        copy.wait_send()
    for k in range(nk):
        z_wait_sends(k)


def write_kernel(*refs):
    n = (len(refs) - 1) // 2
    copies = [pltpu.make_async_copy(refs[i], refs[n + i], refs[-1].at[i]) for i in range(n)]
    for copy in copies:
        copy.start()
    for copy in copies:
        copy.wait()


def write_out(*arrays):
    n = len(arrays)
    return pl.pallas_call(
        write_kernel,
        out_shape=tuple(jax.ShapeDtypeStruct(a.shape, a.dtype) for a in arrays),
        in_specs=[pl.BlockSpec(memory_space=pl.ANY)] * n,
        out_specs=(pl.BlockSpec(memory_space=pltpu.HBM),) * n,
        scratch_shapes=[pltpu.SemaphoreType.DMA((n,))],
        compiler_params=pltpu.CompilerParams(vmem_limit_bytes=4 * 1024 * 1024),
    )(*arrays)


def make_per_device(n_row, n_x, n_zh, n_dp=8):
    def per_device(inputs, weight, cotangent, anchor, first_moment, second_moment):
        T, DR = inputs.shape
        width = weight.shape[1]
        own = DR // n_dp
        nk = len(chunks_of(width))
        hops = max(n_row // 2, 1)
        tall = cotangent.reshape(3, 8, width)
        dma = pltpu.SemaphoreType.DMA
        V = pltpu.VMEM
        scratch = [
            V((T, DR), bf16), V((T, DR), bf16), V((DR, width), bf16),
            V((n_row, 3, 8, width), bf16), V((n_row, 3, 8, width), bf16),
            V((NZ, 2, own, T), bf16), V((NZ * own, T), bf16), V((NZ * own, T), bf16),
            V((NZ * own, width), f32),
            V((n_row, 3, 8, width), bf16), V((2, hops, 3, 8, width), bf16),
            V((T, DR), f32), V((n_zh, n_x, 3, 8, DR), bf16), V((n_x - 1, n_zh, 3, 8, DR), bf16),
            V((3, 8, DR), bf16), V((3, 8, DR), bf16),
            V((NZ, own, width), bf16), V((2, NZ, own, width), bf16), V((own, 512), f32),
            V((own, width), bf16), V((own, width), f32), V((own, width), f32),
            dma((6,)), dma((2,)),
            dma((nk, n_row)), dma((nk, n_row)),
            dma((nk, 2, hops)), dma((nk, 2, hops)),
            dma((2, 2, hops)), dma((2, 2, hops)),
            dma((nk, NZ)), dma((2, nk, NZ)),
            dma((n_x - 1,)), dma((n_x - 1,)), dma((2,)),
            pltpu.SemaphoreType.REGULAR((4,)),
        ]
        hbm = pl.BlockSpec(memory_space=pltpu.HBM)
        results = pl.pallas_call(
            functools.partial(kernel, n_row, n_x, n_zh, T * n_dp),
            out_shape=(
                jax.ShapeDtypeStruct((3, 8, width), bf16),
                jax.ShapeDtypeStruct((3, 8, DR), bf16),
                jax.ShapeDtypeStruct((own, width), bf16),
                jax.ShapeDtypeStruct((own, width), f32),
                jax.ShapeDtypeStruct((own, width), f32),
            ),
            in_specs=[hbm] * 6,
            out_specs=(pl.BlockSpec(memory_space=pltpu.VMEM),) * 5,
            scratch_shapes=scratch,
            compiler_params=pltpu.CompilerParams(
                collective_id=0, has_side_effects=True, vmem_limit_bytes=48 * 1024 * 1024
            ),
        )(*(pltpu.with_memory_space_constraint(a, pltpu.HBM) for a in (inputs, weight, tall, anchor, first_moment, second_moment)))
        return write_out(results[0].reshape(24, width), results[1].reshape(24, DR), *results[2:])

    return per_device


def solution(mesh):
    in_specs = (
        P("dp", "row"),
        P("row", "col"),
        P(("dp", "row"), "col"),
        P(("row", "dp"), "col"),
        P(("row", "dp"), "col"),
        P(("row", "dp"), "col"),
    )
    out_specs = (
        P(("dp", "row"), "col"),
        P(("dp", "col"), "row"),
        P(("row", "dp"), "col"),
        P(("row", "dp"), "col"),
        P(("row", "dp"), "col"),
    )
    n_row, n_col = mesh.shape["row"], mesh.shape["col"]
    n_zh = 2 if n_col > 2 else 1
    return jax.shard_map(
        make_per_device(n_row, n_col // n_zh, n_zh), mesh=mesh,
        in_specs=in_specs, out_specs=out_specs, check_vma=False,
    )
```
